32 devices in a mesh: groups: 2 (over x), epoch: 4 (over y, core), space: 4 (over z).
Axes of the slice: x: 2, y: 2, z: 4, core: 2. Of those that a mesh axis runs over, the one named last changes fastest.
Arguments:
- slc_stack: bfloat16 [2, 32, 32, 960], P(None, ('epoch', 'space'), 'groups'), parts along dimension 2, may hold values from -45 to 45
Outputs:
- coherence: bfloat16 [2, 32, 32, 2048], P(None, 'epoch', None, ('groups', 'space')), parts along dimension 3
The draws below stay inside these ranges and needn't reach their ends.
There are 2 independent parts, one for each index of `groups`. The reference program is written for one: setup_inputs(seed, part) draws one part's arguments, and reference() takes and returns one part's arrays. A program takes and returns all parts, laid end to end along the dimension named above; each array names one. Nothing has to cross between parts.
All inputs are finite; a program needn't handle non-finite values.
Results may differ from the reference program's by a relative error of at most 0.001.
Values may be sent and summed in bfloat16 or wider, within the bound.
No kernel may reach another device: no remote copies, remote signals or barrier semaphores. Data moves between devices by JAX's collectives and lax.ppermute only.
A program may use at most 128 MiB of HBM per device.

```python
import math
import jax
import jax.numpy as jnp
from jax import lax

E = 32
LC = 64
LOOKR = 5
LOOKC = 15
MARGIN = 2
ROWS = 16
COLS = 960


def draw_slc_stack(key, part):
    key_weight, key_common, key_amp, key_noise = jax.random.split(jax.random.fold_in(key, 11), 4)
    weights = jax.random.uniform(key_weight, (1, E, 1, 1), jnp.float32, 0.2, 1.5)
    common = jnp.clip(jax.random.normal(key_common, (2, 1, ROWS, COLS), jnp.float32), -6.0, 6.0)
    amplitude = jnp.exp(jax.random.uniform(key_amp, (1, 1, ROWS, COLS), jnp.float32, math.log(0.3), math.log(3.0)))
    noise = jnp.clip(jax.random.normal(key_noise, (2, E, ROWS, COLS), jnp.float32), -6.0, 6.0)
    return (amplitude * (weights * common + noise)).astype(jnp.bfloat16)


def setup_inputs(seed: int = 0, part: int = 0) -> dict:
    keys = jax.random.split(jax.random.key(seed), 2)
    own_keys = jax.random.split(jax.random.fold_in(keys[1], part), 2)
    return {
        "slc_stack": draw_slc_stack(jax.random.fold_in(jax.random.fold_in(keys[1], part), 71), part),
    }


def window_sums(values_in):
    row_count = values_in.shape[-2] - 2 * MARGIN
    col_count = values_in.shape[-1] // LOOKC
    folded = values_in.reshape(values_in.shape[:-1] + (col_count, LOOKC)).sum(-1)
    running = folded[..., 0:row_count, :]
    for offset in range(1, LOOKR):
        running = running + folded[..., offset:offset + row_count, :]
    return running

def powers_of(strip_data):
    real_part = strip_data[0].astype(jnp.float32)
    imag_part = strip_data[1].astype(jnp.float32)
    return window_sums(real_part * real_part + imag_part * imag_part) + 1e-06

def pair_coherence(left_strip, right_strip, left_power, right_power):
    left_re = left_strip[0].astype(jnp.float32)[:, None]
    left_im = left_strip[1].astype(jnp.float32)[:, None]
    right_re = right_strip[0].astype(jnp.float32)[None]
    right_im = right_strip[1].astype(jnp.float32)[None]
    cross_re = window_sums(left_re * right_re + left_im * right_im)
    cross_im = window_sums(left_im * right_re - left_re * right_im)
    inverse = lax.rsqrt(left_power[:, None] * right_power[None])
    return jnp.stack([cross_re * inverse, cross_im * inverse]).astype(jnp.bfloat16)

def reference(slc_stack):
    padded = jnp.pad(slc_stack, ((0, 0), (0, 0), (MARGIN, MARGIN), (0, 0)))
    power_all = powers_of(padded)

    def one_epoch(epoch_index):
        left_strip = lax.dynamic_slice_in_dim(padded, epoch_index, 1, 1)
        left_power = lax.dynamic_slice_in_dim(power_all, epoch_index, 1, 0)
        return pair_coherence(left_strip, padded, left_power, power_all)[:, 0]
    result = lax.map(one_epoch, jnp.arange(E, dtype=jnp.int32))
    return jnp.transpose(result, (1, 0, 2, 3, 4)).reshape(2, E, E, ROWS * LC)
```

```python
import functools

import jax
import jax.numpy as jnp
from jax import lax
from jax.experimental import pallas as pl
from jax.experimental.pallas import tpu as pltpu
from jax.sharding import PartitionSpec as P

LOOKR = 5
LOOKC = 15
MARGIN = 2
KPAD = 16
LANES = 128
GROUP = 16


def split_kernel(space_count, x_ref, *refs):
    outs, held, turned = refs[:space_count], refs[space_count], refs[space_count + 1]
    parts, epochs, rows, cols = x_ref.shape
    looks = cols // LOOKC
    blocks = looks // GROUP
    width = GROUP * LOOKC
    lines = parts * epochs * rows
    pairs = rows // 2
    planes = parts * epochs
    stride = pairs + MARGIN
    own = lax.axis_index("space")

    x = x_ref[...].reshape(lines, cols)
    source = lax.broadcasted_iota(jnp.int32, (width, 2 * LANES), 0)
    lane = lax.broadcasted_iota(jnp.int32, (width, 2 * LANES), 1)
    word = (lane // GROUP) % 8
    k = 2 * (4 * (lane // LANES) + word % 4) + word // 4
    picks = jnp.where((source == (lane % GROUP) * LOOKC + k) & (k < LOOKC), 1.0, 0.0).astype(jnp.bfloat16)
    turned_blocks = [
        jnp.dot(x[:, j * width : (j + 1) * width], picks, preferred_element_type=jnp.float32)
        for j in range(blocks)
    ]
    lane_row = lax.broadcasted_iota(jnp.int32, (lines, LANES), 1)
    place = (lane_row // GROUP) % 4
    half = lax.broadcasted_iota(jnp.int32, (lines // 2, LANES), 1) < LANES // 2
    zeros = jnp.zeros((KPAD, LANES), jnp.float32)
    for g in range(planes):
        turned[pl.ds(g * stride * KPAD, KPAD), :] = zeros
        turned[pl.ds((g * stride + pairs + 1) * KPAD, KPAD), :] = zeros
    for kp in range(KPAD // 2):
        column = kp // 4
        merged = None
        for j in range(blocks):
            piece = turned_blocks[j][:, column * LANES : (column + 1) * LANES]
            shift = (GROUP * (j - kp % 4)) % LANES
            if shift:
                piece = pltpu.roll(piece, shift, 1)
            merged = piece if merged is None else jnp.where(place == j, piece, merged)
        held[kp] = merged
        even = held[kp, pl.ds(0, lines // 2, stride=2), :]
        odd = held[kp, pl.ds(1, lines // 2, stride=2), :]
        first = jnp.where(half, even, pltpu.roll(odd, LANES // 2, 1))
        second = jnp.where(half, pltpu.roll(even, LANES // 2, 1), odd)
        for offset, value in ((0, first), (1, second)):
            for g in range(planes):
                start = (g * stride + 1) * KPAD + 2 * kp + offset
                turned[pl.ds(start, pairs, stride=KPAD), :] = value[g * pairs : (g + 1) * pairs]
    for j in range(space_count):
        out = outs[j]
        taken = out.shape[2]
        target = own ^ j
        for g in range(planes):
            start = pl.multiple_of((g * stride + target * (taken - MARGIN)) * KPAD, KPAD)
            out[g // epochs, g % epochs] = (
                turned[pl.ds(start, taken * KPAD), :].astype(jnp.bfloat16).reshape(taken, KPAD, LANES)
            )


def windowed(values, h, high):
    a, b, c = values[h], values[h + 1], values[h + 2]
    return a + b + c + pltpu.roll(b + jnp.where(high, a, c), LANES // 2, 1)


def pair_kernel(space_count, block_count, *refs):
    count = space_count * block_count
    pieces, out_ref = refs[:count], refs[count]
    field, sums, own_power = refs[count + 1 :]
    epochs, pairs = pieces[0].shape[1], pieces[0].shape[2]
    group = epochs * space_count
    own = lax.axis_index("space")
    block_own = lax.axis_index("epoch")
    high = lax.broadcasted_iota(jnp.int32, (group, LANES), 1) >= LANES // 2

    for m in range(block_count):
        for j in range(space_count):
            piece = pieces[m * space_count + j]
            for l in range(epochs):
                start = pl.multiple_of(((own ^ j) * epochs + l) * KPAD, KPAD)
                for part in range(2):
                    for q in range(pairs):
                        field[m, part, q, pl.ds(start, KPAD), :] = piece[part, l, q].astype(jnp.float32)

    def block(m, carry):
        def strip(q, power_carry):
            re_sum = [jnp.zeros((group, LANES), jnp.float32) for _ in range(group)]
            im_sum = [jnp.zeros((group, LANES), jnp.float32) for _ in range(group)]
            power = jnp.zeros((group, LANES), jnp.float32)
            for k in range(LOOKC):
                right_re = field[m, 0, q, pl.ds(k, group, stride=KPAD), :]
                right_im = field[m, 1, q, pl.ds(k, group, stride=KPAD), :]
                power = power + (right_re * right_re + right_im * right_im)
                for e in range(group):
                    left_re = field[0, 0, q, pl.ds(e * KPAD + k, 1), :]
                    left_im = field[0, 1, q, pl.ds(e * KPAD + k, 1), :]
                    re_sum[e] = re_sum[e] + (left_re * right_re + left_im * right_im)
                    im_sum[e] = im_sum[e] + (left_im * right_re - left_re * right_im)
            for e in range(group):
                sums[q, 0, e] = re_sum[e]
                sums[q, 1, e] = im_sum[e]
            sums[q, 0, group] = power
            return power_carry

        lax.fori_loop(0, pairs, strip, 0)
        row = pl.multiple_of((block_own ^ m) * group, group)
        for h in range(pairs - MARGIN):
            power = windowed([sums[q, 0, group] for q in range(pairs)], h, high) + 1e-06

            @pl.when(m == 0)
            def _():
                own_power[h] = power

            for e in range(group):
                inverse = lax.rsqrt(own_power[h, pl.ds(e, 1), :] * power)
                for part in range(2):
                    cross = windowed([sums[q, part, e] for q in range(pairs)], h, high)
                    out_ref[part, e, pl.ds(row, group), h * LANES : (h + 1) * LANES] = (
                        cross * inverse
                    ).astype(jnp.bfloat16)
        return carry

    lax.fori_loop(0, block_count, block, 0)


def swapped(value, axis, mask):
    count = lax.axis_size(axis)
    return lax.ppermute(value, axis, [(a, a ^ mask) for a in range(count)])


def per_device(slc_stack):
    parts, epochs, rows, cols = slc_stack.shape
    space_count = lax.axis_size("space")
    epoch_count = lax.axis_size("epoch")
    strip_rows = rows // space_count
    looks = cols // LOOKC
    pairs = strip_rows // 2 + MARGIN
    group = epochs * space_count
    planes = parts * epochs
    vmem = pl.BlockSpec(memory_space=pltpu.VMEM)
    piece_shape = (parts, epochs, pairs, KPAD, LANES)

    strips = pl.pallas_call(
        functools.partial(split_kernel, space_count),
        out_shape=[jax.ShapeDtypeStruct(piece_shape, jnp.bfloat16)] * space_count,
        in_specs=[vmem],
        out_specs=[vmem] * space_count,
        scratch_shapes=[
            pltpu.VMEM((KPAD // 2, planes * rows, LANES), jnp.float32),
            pltpu.VMEM((planes * (rows // 2 + MARGIN) * KPAD, LANES), jnp.float32),
        ],
        name="split",
    )(slc_stack)

    pieces = [strips[0]] + [swapped(strips[j], "space", j) for j in range(1, space_count)]
    blocks = {0: pieces}
    bit = epoch_count // 2
    while bit:
        for mask in list(blocks):
            blocks[mask | bit] = [swapped(p, "epoch", bit) for p in blocks[mask]]
        bit //= 2
    operands = [p for m in range(epoch_count) for p in blocks[m]]

    out_shape = (2, group, group * epoch_count, strip_rows * looks)
    return pl.pallas_call(
        functools.partial(pair_kernel, space_count, epoch_count),
        out_shape=jax.ShapeDtypeStruct(out_shape, jnp.bfloat16),
        in_specs=[vmem] * len(operands),
        out_specs=vmem,
        scratch_shapes=[
            pltpu.VMEM((epoch_count, 2, pairs, group * KPAD, LANES), jnp.float32),
            pltpu.VMEM((pairs, 2, group + 1, group, LANES), jnp.float32),
            pltpu.VMEM((pairs - MARGIN, group, LANES), jnp.float32),
        ],
        name="pairs",
    )(*operands)


def solution(mesh):
    in_specs = (P(None, ("epoch", "space"), "groups", None),)
    out_specs = P(None, "epoch", None, ("groups", "space"))
    return jax.shard_map(
        per_device, mesh=mesh, in_specs=in_specs, out_specs=out_specs, check_vma=False
    )
```

```python
import functools

import jax
import jax.numpy as jnp
from jax import lax
from jax.experimental import pallas as pl
from jax.experimental.pallas import tpu as pltpu
from jax.sharding import PartitionSpec as P

LOOKR = 5
LOOKC = 15
MARGIN = 2
KPAD = 16
LANES = 128
GROUP = 16
GRANT = 6 << 20


def split_kernel(space_count, x_ref, *refs):
    outs, held, turned = refs[:space_count], refs[space_count], refs[space_count + 1]
    parts, epochs, rows, cols = x_ref.shape
    looks = cols // LOOKC
    blocks = looks // GROUP
    width = GROUP * LOOKC
    lines = parts * epochs * rows
    pairs = rows // 2
    planes = parts * epochs
    stride = pairs + MARGIN
    own = lax.axis_index("space")

    x = x_ref[...].reshape(lines, cols)
    source = lax.broadcasted_iota(jnp.int32, (width, 2 * LANES), 0)
    lane = lax.broadcasted_iota(jnp.int32, (width, 2 * LANES), 1)
    word = (lane // GROUP) % 8
    k = 2 * (4 * (lane // LANES) + word % 4) + word // 4
    picks = jnp.where((source == (lane % GROUP) * LOOKC + k) & (k < LOOKC), 1.0, 0.0).astype(jnp.bfloat16)
    turned_blocks = [
        jnp.dot(x[:, j * width : (j + 1) * width], picks, preferred_element_type=jnp.float32)
        for j in range(blocks)
    ]
    lane_row = lax.broadcasted_iota(jnp.int32, (lines, LANES), 1)
    place = (lane_row // GROUP) % 4
    half = lax.broadcasted_iota(jnp.int32, (lines // 2, LANES), 1) < LANES // 2
    zeros = jnp.zeros((KPAD, LANES), jnp.float32)
    for g in range(planes):
        turned[pl.ds(g * stride * KPAD, KPAD), :] = zeros
        turned[pl.ds((g * stride + pairs + 1) * KPAD, KPAD), :] = zeros
    for kp in range(KPAD // 2):
        column = kp // 4
        merged = None
        for j in range(blocks):
            piece = turned_blocks[j][:, column * LANES : (column + 1) * LANES]
            shift = (GROUP * (j - kp % 4)) % LANES
            if shift:
                piece = pltpu.roll(piece, shift, 1)
            merged = piece if merged is None else jnp.where(place == j, piece, merged)
        held[kp] = merged
        even = held[kp, pl.ds(0, lines // 2, stride=2), :]
        odd = held[kp, pl.ds(1, lines // 2, stride=2), :]
        first = jnp.where(half, even, pltpu.roll(odd, LANES // 2, 1))
        second = jnp.where(half, pltpu.roll(even, LANES // 2, 1), odd)
        for offset, value in ((0, first), (1, second)):
            for g in range(planes):
                start = (g * stride + 1) * KPAD + 2 * kp + offset
                turned[pl.ds(start, pairs, stride=KPAD), :] = value[g * pairs : (g + 1) * pairs]
    for j in range(space_count):
        out = outs[j]
        taken = out.shape[2]
        target = own ^ j
        for g in range(planes):
            start = pl.multiple_of((g * stride + target * (taken - MARGIN)) * KPAD, KPAD)
            out[g // epochs, g % epochs] = (
                turned[pl.ds(start, taken * KPAD), :].astype(jnp.bfloat16).reshape(taken, KPAD, LANES)
            )


def windowed(values, h, high):
    a, b, c = values[h], values[h + 1], values[h + 2]
    return a + b + c + pltpu.roll(b + jnp.where(high, a, c), LANES // 2, 1)


def spread(pieces, field, own, epochs):
    pairs = pieces[0].shape[2]
    for j, piece in enumerate(pieces):
        for l in range(epochs):
            start = pl.multiple_of(((own ^ j) * epochs + l) * KPAD, KPAD)
            for part in range(2):
                for q in range(pairs):
                    field[part, q, pl.ds(start, KPAD), :] = piece[part, l, q].astype(jnp.float32)


def pair_kernel(space_count, mask, *refs):
    pieces, refs = refs[:space_count], refs[space_count:]
    epochs, pairs = pieces[0].shape[1], pieces[0].shape[2]
    group = epochs * space_count
    if mask:
        left, own_power, _, out_hbm, right, sums, staged, sem = refs
    else:
        out_hbm, left, own_power, sums, staged, sem = refs
        right = left
    spread(pieces, right, lax.axis_index("space"), epochs)
    high = lax.broadcasted_iota(jnp.int32, (group, LANES), 1) >= LANES // 2

    def strip(q, carry):
        re_sum = [jnp.zeros((group, LANES), jnp.float32) for _ in range(group)]
        im_sum = [jnp.zeros((group, LANES), jnp.float32) for _ in range(group)]
        power = jnp.zeros((group, LANES), jnp.float32)
        for k in range(LOOKC):
            right_re = right[0, q, pl.ds(k, group, stride=KPAD), :]
            right_im = right[1, q, pl.ds(k, group, stride=KPAD), :]
            power = power + (right_re * right_re + right_im * right_im)
            for e in range(group):
                left_re = left[0, q, pl.ds(e * KPAD + k, 1), :]
                left_im = left[1, q, pl.ds(e * KPAD + k, 1), :]
                re_sum[e] = re_sum[e] + (left_re * right_re + left_im * right_im)
                im_sum[e] = im_sum[e] + (left_im * right_re - left_re * right_im)
        for e in range(group):
            sums[q, 0, e] = re_sum[e]
            sums[q, 1, e] = im_sum[e]
        sums[q, 0, group] = power
        return carry

    lax.fori_loop(0, pairs, strip, 0)
    for h in range(pairs - MARGIN):
        power = windowed([sums[q, 0, group] for q in range(pairs)], h, high) + 1e-06
        if mask == 0:
            own_power[h] = power
        for e in range(group):
            inverse = lax.rsqrt(own_power[h, pl.ds(e, 1), :] * power)
            for part in range(2):
                cross = windowed([sums[q, part, e] for q in range(pairs)], h, high)
                staged[part, e, :, h * LANES : (h + 1) * LANES] = (cross * inverse).astype(jnp.bfloat16)
    row = pl.multiple_of((lax.axis_index("epoch") ^ mask) * group, group)
    copy = pltpu.make_async_copy(staged, out_hbm.at[:, :, pl.ds(row, group), :], sem)
    copy.start()
    copy.wait()


def swapped(value, axis, mask):
    count = lax.axis_size(axis)
    return lax.ppermute(value, axis, [(a, a ^ mask) for a in range(count)])


def per_device(slc_stack):
    parts, epochs, rows, cols = slc_stack.shape
    space_count = lax.axis_size("space")
    epoch_count = lax.axis_size("epoch")
    strip_rows = rows // space_count
    looks = cols // LOOKC
    pairs = strip_rows // 2 + MARGIN
    group = epochs * space_count
    planes = parts * epochs
    vmem = pl.BlockSpec(memory_space=pltpu.VMEM)
    piece_shape = (parts, epochs, pairs, KPAD, LANES)

    strips = pl.pallas_call(
        functools.partial(split_kernel, space_count),
        out_shape=[jax.ShapeDtypeStruct(piece_shape, jnp.bfloat16)] * space_count,
        in_specs=[vmem],
        out_specs=[vmem] * space_count,
        scratch_shapes=[
            pltpu.VMEM((KPAD // 2, planes * rows, LANES), jnp.float32),
            pltpu.VMEM((planes * (rows // 2 + MARGIN) * KPAD, LANES), jnp.float32),
        ],
        compiler_params=pltpu.CompilerParams(vmem_limit_bytes=GRANT),
        name="split",
    )(slc_stack)

    pieces = [strips[0]] + [swapped(strips[j], "space", j) for j in range(1, space_count)]
    blocks = {0: pieces}
    order = []
    bit = epoch_count // 2
    while bit:
        for mask in list(blocks):
            blocks[mask | bit] = [swapped(p, "epoch", bit) for p in blocks[mask]]
            order.append(mask | bit)
        bit //= 2
    order.sort(key=lambda mask: (bin(mask).count("1"), mask))
    field_shape = jax.ShapeDtypeStruct((2, pairs, group * KPAD, LANES), jnp.float32)
    power_shape = jax.ShapeDtypeStruct((pairs - MARGIN, group, LANES), jnp.float32)
    out_shape = jax.ShapeDtypeStruct((2, group, group * epoch_count, strip_rows * looks), jnp.bfloat16)
    anywhere = pl.BlockSpec(memory_space=pl.ANY)
    common = [
        pltpu.VMEM((pairs, 2, group + 1, group, LANES), jnp.float32),
        pltpu.VMEM((2, group, group, strip_rows * looks), jnp.bfloat16),
        pltpu.SemaphoreType.DMA,
    ]
    params = pltpu.CompilerParams(vmem_limit_bytes=GRANT)
    cost = pl.CostEstimate(
        flops=8 * group * group * pairs * LOOKC * LANES,
        bytes_accessed=space_count * parts * epochs * pairs * KPAD * LANES * 2,
        transcendentals=group * group * strip_rows * looks,
    )
    out, left, power = pl.pallas_call(
        functools.partial(pair_kernel, space_count, 0),
        out_shape=[out_shape, field_shape, power_shape],
        in_specs=[vmem] * space_count,
        out_specs=[anywhere, vmem, vmem],
        scratch_shapes=common,
        compiler_params=params,
        cost_estimate=cost,
        name="pairs_0",
    )(*blocks[0])
    for mask in order:
        out = pl.pallas_call(
            functools.partial(pair_kernel, space_count, mask),
            out_shape=out_shape,
            in_specs=[vmem] * (space_count + 2) + [anywhere],
            out_specs=anywhere,
            input_output_aliases={space_count + 2: 0},
            scratch_shapes=[pltpu.VMEM(field_shape.shape, jnp.float32)] + common,
            compiler_params=params,
            cost_estimate=cost,
            name=f"pairs_{mask}",
        )(*blocks[mask], left, power, out)
    return out


def solution(mesh):
    in_specs = (P(None, ("epoch", "space"), "groups", None),)
    out_specs = P(None, "epoch", None, ("groups", "space"))
    return jax.shard_map(
        per_device, mesh=mesh, in_specs=in_specs, out_specs=out_specs, check_vma=False
    )
```

```python
import functools

import jax
import jax.numpy as jnp
from jax import lax
from jax.experimental import pallas as pl
from jax.experimental.pallas import tpu as pltpu
from jax.sharding import PartitionSpec as P

LOOKC = 15
MARGIN = 2
KPAD = 16
LANES = 128
GROUP = 16
GRANT = 6 << 20


def split_kernel(space_count, x_ref, *refs):
    outs, held, turned = refs[:space_count], refs[space_count], refs[space_count + 1]
    parts, epochs, rows, cols = x_ref.shape
    looks = cols // LOOKC
    blocks = looks // GROUP
    width = GROUP * LOOKC
    lines = parts * epochs * rows
    pairs = rows // 2
    planes = parts * epochs
    stride = pairs + MARGIN
    own = lax.axis_index("space")

    x = x_ref[...].reshape(lines, cols)
    source = lax.broadcasted_iota(jnp.int32, (width, 2 * LANES), 0)
    lane = lax.broadcasted_iota(jnp.int32, (width, 2 * LANES), 1)
    word = (lane // GROUP) % 8
    k = 2 * (4 * (lane // LANES) + word % 4) + word // 4
    picks = jnp.where((source == (lane % GROUP) * LOOKC + k) & (k < LOOKC), 1.0, 0.0).astype(jnp.bfloat16)
    turned_blocks = [
        jnp.dot(x[:, j * width : (j + 1) * width], picks, preferred_element_type=jnp.float32)
        for j in range(blocks)
    ]
    lane_row = lax.broadcasted_iota(jnp.int32, (lines, LANES), 1)
    place = (lane_row // GROUP) % 4
    half = lax.broadcasted_iota(jnp.int32, (lines // 2, LANES), 1) < LANES // 2
    zeros = jnp.zeros((KPAD, LANES), jnp.float32)
    for g in range(planes):
        turned[pl.ds(g * stride * KPAD, KPAD), :] = zeros
        turned[pl.ds((g * stride + pairs + 1) * KPAD, KPAD), :] = zeros
    for kp in range(KPAD // 2):
        column = kp // 4
        merged = None
        for j in range(blocks):
            piece = turned_blocks[j][:, column * LANES : (column + 1) * LANES]
            shift = (GROUP * (j - kp % 4)) % LANES
            if shift:
                piece = pltpu.roll(piece, shift, 1)
            merged = piece if merged is None else jnp.where(place == j, piece, merged)
        held[kp] = merged
        even = held[kp, pl.ds(0, lines // 2, stride=2), :]
        odd = held[kp, pl.ds(1, lines // 2, stride=2), :]
        first = jnp.where(half, even, pltpu.roll(odd, LANES // 2, 1))
        second = jnp.where(half, pltpu.roll(even, LANES // 2, 1), odd)
        for offset, value in ((0, first), (1, second)):
            for g in range(planes):
                start = (g * stride + 1) * KPAD + 2 * kp + offset
                turned[pl.ds(start, pairs, stride=KPAD), :] = value[g * pairs : (g + 1) * pairs]
    for j in range(space_count):
        out = outs[j]
        taken = out.shape[2]
        target = own ^ j
        for g in range(planes):
            start = pl.multiple_of((g * stride + target * (taken - MARGIN)) * KPAD, KPAD)
            out[g // epochs, g % epochs] = (
                turned[pl.ds(start, taken * KPAD), :].astype(jnp.bfloat16).reshape(taken, KPAD, LANES)
            )


def windowed(values, h, high):
    a, b, c = values[h], values[h + 1], values[h + 2]
    return a + b + c + pltpu.roll(b + jnp.where(high, a, c), LANES // 2, 1)


def spread(pieces, field, own, epochs):
    pairs = pieces[0].shape[2]
    for j, piece in enumerate(pieces):
        for l in range(epochs):
            start = pl.multiple_of(((own ^ j) * epochs + l) * KPAD, KPAD)
            for part in range(2):
                for q in range(pairs):
                    field[part, q, pl.ds(start, KPAD), :] = piece[part, l, q].astype(jnp.float32)


def pair_kernel(space_count, mask, *refs):
    pieces, refs = refs[:space_count], refs[space_count:]
    epochs, pairs = pieces[0].shape[1], pieces[0].shape[2]
    group = epochs * space_count
    if mask:
        left, own_power, _, out_hbm, right, sums, staged, sem = refs
    else:
        out_hbm, left, own_power, sums, staged, sem = refs
        right = left
    spread(pieces, right, lax.axis_index("space"), epochs)
    high = lax.broadcasted_iota(jnp.int32, (group, LANES), 1) >= LANES // 2

    def strip(q, carry):
        re_sum = [jnp.zeros((group, LANES), jnp.float32) for _ in range(group)]
        im_sum = [jnp.zeros((group, LANES), jnp.float32) for _ in range(group)]
        power = jnp.zeros((group, LANES), jnp.float32)
        for k in range(LOOKC):
            right_re = right[0, q, pl.ds(k, group, stride=KPAD), :]
            right_im = right[1, q, pl.ds(k, group, stride=KPAD), :]
            power = power + (right_re * right_re + right_im * right_im)
            for e in range(group):
                left_re = left[0, q, pl.ds(e * KPAD + k, 1), :]
                left_im = left[1, q, pl.ds(e * KPAD + k, 1), :]
                re_sum[e] = re_sum[e] + (left_re * right_re + left_im * right_im)
                im_sum[e] = im_sum[e] + (left_im * right_re - left_re * right_im)
        for e in range(group):
            sums[q, 0, e] = re_sum[e]
            sums[q, 1, e] = im_sum[e]
        sums[q, 0, group] = power
        return carry

    lax.fori_loop(0, pairs, strip, 0)
    for h in range(pairs - MARGIN):
        power = windowed([sums[q, 0, group] for q in range(pairs)], h, high) + 1e-06
        if mask == 0:
            own_power[h] = power
        for e in range(group):
            inverse = lax.rsqrt(own_power[h, pl.ds(e, 1), :] * power)
            for part in range(2):
                cross = windowed([sums[q, part, e] for q in range(pairs)], h, high)
                staged[part, e, :, h * LANES : (h + 1) * LANES] = (cross * inverse).astype(jnp.bfloat16)
    row = pl.multiple_of((lax.axis_index("epoch") ^ mask) * group, group)
    copy = pltpu.make_async_copy(staged, out_hbm.at[:, :, pl.ds(row, group), :], sem)
    copy.start()
    copy.wait()


def swapped(value, axis, mask):
    count = lax.axis_size(axis)
    return lax.ppermute(value, axis, [(a, a ^ mask) for a in range(count)])


def per_device(slc_stack):
    parts, epochs, rows, cols = slc_stack.shape
    space_count = lax.axis_size("space")
    epoch_count = lax.axis_size("epoch")
    strip_rows = rows // space_count
    looks = cols // LOOKC
    pairs = strip_rows // 2 + MARGIN
    group = epochs * space_count
    planes = parts * epochs
    vmem = pl.BlockSpec(memory_space=pltpu.VMEM)
    piece_shape = (parts, epochs, pairs, KPAD, LANES)

    strips = pl.pallas_call(
        functools.partial(split_kernel, space_count),
        out_shape=[jax.ShapeDtypeStruct(piece_shape, jnp.bfloat16)] * space_count,
        in_specs=[vmem],
        out_specs=[vmem] * space_count,
        scratch_shapes=[
            pltpu.VMEM((KPAD // 2, planes * rows, LANES), jnp.float32),
            pltpu.VMEM((planes * (rows // 2 + MARGIN) * KPAD, LANES), jnp.float32),
        ],
        compiler_params=pltpu.CompilerParams(vmem_limit_bytes=GRANT),
        name="split",
    )(slc_stack)

    pieces = [strips[0]] + [swapped(strips[j], "space", j) for j in range(1, space_count)]
    blocks = {0: pieces}
    order = []
    bit = epoch_count // 2
    while bit:
        for mask in list(blocks):
            blocks[mask | bit] = [swapped(p, "epoch", bit) for p in blocks[mask]]
            order.append(mask | bit)
        bit //= 2
    order.sort(key=lambda mask: (bin(mask).count("1"), mask))
    field_shape = jax.ShapeDtypeStruct((2, pairs, group * KPAD, LANES), jnp.float32)
    power_shape = jax.ShapeDtypeStruct((pairs - MARGIN, group, LANES), jnp.float32)
    out_shape = jax.ShapeDtypeStruct((2, group, group * epoch_count, strip_rows * looks), jnp.bfloat16)
    anywhere = pl.BlockSpec(memory_space=pl.ANY)
    common = [
        pltpu.VMEM((pairs, 2, group + 1, group, LANES), jnp.float32),
        pltpu.VMEM((2, group, group, strip_rows * looks), jnp.bfloat16),
        pltpu.SemaphoreType.DMA,
    ]
    params = pltpu.CompilerParams(vmem_limit_bytes=GRANT)
    cost = pl.CostEstimate(
        flops=8 * group * group * pairs * LOOKC * LANES,
        bytes_accessed=space_count * parts * epochs * pairs * KPAD * LANES * 2,
        transcendentals=group * group * strip_rows * looks,
    )
    out, left, power = pl.pallas_call(
        functools.partial(pair_kernel, space_count, 0),
        out_shape=[out_shape, field_shape, power_shape],
        in_specs=[vmem] * space_count,
        out_specs=[anywhere, vmem, vmem],
        scratch_shapes=common,
        compiler_params=params,
        cost_estimate=cost,
        name="pairs_0",
    )(*blocks[0])
    for mask in order:
        out = pl.pallas_call(
            functools.partial(pair_kernel, space_count, mask),
            out_shape=out_shape,
            in_specs=[vmem] * (space_count + 2) + [anywhere],
            out_specs=anywhere,
            input_output_aliases={space_count + 2: 0},
            scratch_shapes=[pltpu.VMEM(field_shape.shape, jnp.float32)] + common,
            compiler_params=params,
            cost_estimate=cost,
        )(*blocks[mask], left, power, out)
    return out


def solution(mesh):
    in_specs = (P(None, ("epoch", "space"), "groups", None),)
    out_specs = P(None, "epoch", None, ("groups", "space"))

    return jax.shard_map(per_device, mesh=mesh, in_specs=in_specs, out_specs=out_specs, check_vma=False)
```

```python
import functools

import jax
import jax.numpy as jnp
from jax import lax
from jax.experimental import pallas as pl
from jax.experimental.pallas import tpu as pltpu
from jax.sharding import PartitionSpec as P

LOOKC = 15
MARGIN = 2
LANES = 128
SUBLANES = 8
GROUP = 16
GRANT = 8 << 20


def split_kernel(space_count, x_ref, *refs):
    outs, held, turned = refs[:space_count], refs[space_count], refs[space_count + 1]
    parts, epochs, rows, cols = x_ref.shape
    looks = cols // LOOKC
    blocks = looks // GROUP
    width = GROUP * LOOKC
    lines = parts * epochs * rows
    pairs = rows // 2
    own = lax.axis_index("space")

    x = x_ref[...].reshape(lines, cols)
    source = lax.broadcasted_iota(jnp.int32, (width, 2 * LANES), 0)
    lane = lax.broadcasted_iota(jnp.int32, (width, 2 * LANES), 1)
    word = (lane // GROUP) % 8
    k = 2 * (4 * (lane // LANES) + word % 4) + word // 4
    picks = jnp.where((source == (lane % GROUP) * LOOKC + k) & (k < LOOKC), 1.0, 0.0).astype(jnp.bfloat16)
    turned_blocks = [
        jnp.dot(x[:, j * width : (j + 1) * width], picks, preferred_element_type=jnp.float32)
        for j in range(blocks)
    ]
    place = (lax.broadcasted_iota(jnp.int32, (lines, LANES), 1) // GROUP) % 4
    half = lax.broadcasted_iota(jnp.int32, (lines // 2, LANES), 1) < LANES // 2
    zeros = jnp.zeros((SUBLANES, LANES), jnp.float32)
    for kp in range((LOOKC + 1) // 2):
        column = kp // 4
        merged = None
        for j in range(blocks):
            piece = turned_blocks[j][:, column * LANES : (column + 1) * LANES]
            shift = (GROUP * (j - kp % 4)) % LANES
            if shift:
                piece = pltpu.roll(piece, shift, 1)
            merged = piece if merged is None else jnp.where(place == j, piece, merged)
        held[kp] = merged
        even = held[kp, pl.ds(0, lines // 2, stride=2), :]
        odd = held[kp, pl.ds(1, lines // 2, stride=2), :]
        first = jnp.where(half, even, pltpu.roll(odd, LANES // 2, 1))
        second = jnp.where(half, pltpu.roll(even, LANES // 2, 1), odd)
        for at, value in ((2 * kp, first), (2 * kp + 1, second)):
            if at >= LOOKC:
                continue
            for part in range(parts):
                for l in range(epochs):
                    g = part * epochs + l
                    turned[part, at, l, 0:SUBLANES, :] = zeros
                    turned[part, at, l, SUBLANES : SUBLANES + pairs, :] = value[g * pairs : (g + 1) * pairs]
                    turned[part, at, l, SUBLANES + pairs : 2 * SUBLANES + pairs, :] = zeros
    taken = outs[0].shape[2] // epochs
    for j in range(space_count):
        start = SUBLANES - 1 + (own ^ j) * (taken - MARGIN)
        for part in range(parts):
            for at in range(LOOKC):
                tile = [turned[part, at, l, pl.ds(start, taken), :] for l in range(epochs)]
                tile = tile[0] if epochs == 1 else jnp.concatenate(tile, axis=0)
                outs[j][part, at] = tile.astype(jnp.bfloat16)


def windowed(values, h, high):
    a, b, c = values[h], values[h + 1], values[h + 2]
    return a + b + c + pltpu.roll(b + jnp.where(high, a, c), LANES // 2, 1)


def stage_kernel(plan, *refs):
    space_count, epochs, taken = plan["space"], plan["epochs"], plan["taken"]
    build, tasks, finish, first, last = (plan[n] for n in ("build", "tasks", "finish", "first", "last"))
    names = sorted(set([(0, j) for j in build] + [(m, j) for m, j, _ in tasks]))
    pieces = dict(zip(names, refs[: len(names)]))
    refs = refs[len(names) :]
    if not first:
        refs = refs[4:]
    if last:
        out_hbm, refs = refs[0], refs[1:]
    left, sums, powers, ready = refs[:4]
    own_power = refs[4]
    group = epochs * space_count
    lines = epochs * taken
    own = lax.axis_index("space")
    block_own = lax.axis_index("epoch")
    blocks = ready.shape[0]

    def send(m):
        row = pl.multiple_of((block_own ^ m) * group, group)
        return pltpu.make_async_copy(ready.at[m], out_hbm.at[:, :, pl.ds(row, group), :], refs[5].at[m])

    if last:
        for m in range(blocks):
            if m not in finish:
                send(m).start()

    for j in build:
        piece = pieces[0, j]

        def lift(k, carry):
            for part in range(2):
                tile = piece[part, k].astype(jnp.float32)
                for l in range(epochs):
                    half = tile[l * taken : (l + 1) * taken]
                    if epochs > 1:
                        half = jnp.concatenate([half] * epochs, axis=0)
                    left[k, part, (own ^ j) * epochs + l] = half
            return carry

        lax.fori_loop(0, LOOKC, lift, 0)

    for m, j, sources in tasks:
        piece = pieces[m, j]
        chosen = [(own ^ s) * epochs + l for s in sources for l in range(epochs)]
        count = len(chosen)
        zero = jnp.zeros((lines, LANES), jnp.float32)

        def add(step, carry):
            carry = list(carry)
            for inner in range(3):
                k = step * 3 + inner
                right_re = piece[0, k].astype(jnp.float32)
                right_im = piece[1, k].astype(jnp.float32)
                carry[2 * count] = carry[2 * count] + (right_re * right_re + right_im * right_im)
                for n, e in enumerate(chosen):
                    left_re = left[k, 0, e]
                    left_im = left[k, 1, e]
                    carry[2 * n] = carry[2 * n] + (left_re * right_re + left_im * right_im)
                    carry[2 * n + 1] = carry[2 * n + 1] + (left_im * right_re - left_re * right_im)
            return tuple(carry)

        total = lax.fori_loop(0, LOOKC // 3, add, (zero,) * (2 * count + 1))
        row = pl.multiple_of((own ^ j) * SUBLANES, SUBLANES)
        for n, e in enumerate(chosen):
            for part in range(2):
                sums[m, part, e, pl.ds(row, lines), :] = total[2 * n + part]
        powers[m, pl.ds(row, lines), :] = total[2 * count]

    stride = SUBLANES // epochs
    high = lax.broadcasted_iota(jnp.int32, (group, LANES), 1) >= LANES // 2

    def power_of(m, h):
        return windowed([powers[m, pl.ds(q, group, stride=stride), :] for q in range(taken)], h, high) + 1e-06

    if finish:
        for h in range(taken - MARGIN):
            own_power[h] = power_of(0, h)
    for m in finish:
        power = [power_of(m, h) for h in range(taken - MARGIN)]
        for e in range(group):
            inverse = [lax.rsqrt(own_power[h, pl.ds(e, 1), :] * power[h]) for h in range(taken - MARGIN)]
            for part in range(2):
                values = [sums[m, part, e, pl.ds(q, group, stride=stride), :] for q in range(taken)]
                for h in range(taken - MARGIN):
                    ready[m, part, e, :, h * LANES : (h + 1) * LANES] = (
                        windowed(values, h, high) * inverse[h]
                    ).astype(jnp.bfloat16)
        if last:
            send(m).start()
    if last:
        for m in range(blocks):
            send(m).wait()


def swapped(value, axis, mask):
    count = lax.axis_size(axis)
    return lax.ppermute(value, axis, [(a, a ^ mask) for a in range(count)])


def stages_of(space_count, epoch_count, order):
    every = tuple(range(space_count))
    if space_count == 4 and epoch_count == 4:
        return [[(int(n[0]), int(n[1]), tuple(map(int, n[2:])) or every) for n in stage] for stage in STAGES]
    return [[(m, j, every) for j in every] for m in [0] + order]


def per_device(slc_stack):
    parts, epochs, rows, cols = slc_stack.shape
    space_count = lax.axis_size("space")
    epoch_count = lax.axis_size("epoch")
    strip_rows = rows // space_count
    looks = cols // LOOKC
    taken = strip_rows // 2 + MARGIN
    group = epochs * space_count
    lines = epochs * taken
    vmem = pl.BlockSpec(memory_space=pltpu.VMEM)
    params = pltpu.CompilerParams(vmem_limit_bytes=GRANT)

    strips = pl.pallas_call(
        functools.partial(split_kernel, space_count),
        out_shape=[jax.ShapeDtypeStruct((parts, LOOKC, lines, LANES), jnp.bfloat16)] * space_count,
        in_specs=[vmem],
        out_specs=[vmem] * space_count,
        scratch_shapes=[
            pltpu.VMEM(((LOOKC + 1) // 2, parts * epochs * rows, LANES), jnp.float32),
            pltpu.VMEM((parts, LOOKC, epochs, rows // 2 + 2 * SUBLANES, LANES), jnp.float32),
        ],
        compiler_params=params,
        name="split",
    )(slc_stack)

    blocks = {0: [strips[0]] + [swapped(strips[j], "space", j) for j in range(1, space_count)]}
    order = []
    bit = epoch_count // 2
    while bit:
        for mask in list(blocks):
            blocks[mask | bit] = [swapped(p, "epoch", bit) for p in blocks[mask]]
            order.append(mask | bit)
        bit //= 2
    order.sort(key=lambda mask: (bin(mask).count("1"), mask))

    state_shapes = [
        jax.ShapeDtypeStruct((LOOKC, parts, group, lines, LANES), jnp.float32),
        jax.ShapeDtypeStruct((epoch_count, parts, group, space_count * SUBLANES, LANES), jnp.float32),
        jax.ShapeDtypeStruct((epoch_count, space_count * SUBLANES, LANES), jnp.float32),
        jax.ShapeDtypeStruct((epoch_count, parts, group, group, strip_rows * looks), jnp.bfloat16),
    ]
    out_shape = jax.ShapeDtypeStruct((parts, group, group * epoch_count, strip_rows * looks), jnp.bfloat16)
    stages = stages_of(space_count, epoch_count, order)
    built, done, finished = set(), set(), set()
    state = ()
    out = None
    for number, tasks in enumerate(stages):
        first, last = number == 0, number == len(stages) - 1
        build = sorted({s for _, _, sources in tasks for s in sources} - built)
        built |= set(build)
        done |= {(m, j, s) for m, j, sources in tasks for s in sources}
        full = [
            m
            for m in [0] + order
            if all((m, j, s) in done for j in range(space_count) for s in range(space_count))
        ]
        finish = [m for m in full if m not in finished] if 0 in full else []
        finished |= set(finish)
        plan = dict(
            space=space_count, epochs=epochs, taken=taken, build=build, tasks=tasks, finish=finish,
            first=first, last=last,
        )
        names = sorted(set([(0, j) for j in build] + [(m, j) for m, j, _ in tasks]))
        work = sum(len(sources) for _, _, sources in tasks)
        results = pl.pallas_call(
            functools.partial(stage_kernel, plan),
            out_shape=([out_shape] if last else []) + state_shapes,
            in_specs=[vmem] * (len(names) + len(state)),
            out_specs=([pl.BlockSpec(memory_space=pl.ANY)] if last else []) + [vmem] * 4,
            input_output_aliases={len(names) + n: n + int(last) for n in range(len(state))},
            scratch_shapes=[pltpu.VMEM((taken - MARGIN, group, LANES), jnp.float32)]
            + ([pltpu.SemaphoreType.DMA((epoch_count,))] if last else []),
            compiler_params=params,
            cost_estimate=pl.CostEstimate(
                flops=8 * work * epochs * lines * LOOKC * LANES,
                bytes_accessed=len(names) * parts * LOOKC * lines * LANES * 2,
                transcendentals=0,
            ),
        )(*[blocks[m][j] for m, j in names], *state)
        if last:
            out, results = results[0], results[1:]
        state = tuple(results)
    return out


STAGES = (
    ("00", "01", "02", "03", "20", "21", "10", "11"),
    ("12", "13", "22", "23", "30", "31", "32"),
    ("33",),
)


def solution(mesh):
    in_specs = (P(None, ("epoch", "space"), "groups", None),)
    out_specs = P(None, "epoch", None, ("groups", "space"))

    return jax.shard_map(per_device, mesh=mesh, in_specs=in_specs, out_specs=out_specs, check_vma=False)
```

```python
import functools

import jax
import jax.numpy as jnp
from jax import lax
from jax.experimental import pallas as pl
from jax.experimental.pallas import tpu as pltpu
from jax.sharding import PartitionSpec as P

LOOKC = 15
MARGIN = 2
LANES = 128
SUBLANES = 8
GROUP = 16
GRANT = 8 << 20


def split_kernel(space_count, x_hbm, *refs):
    outs = refs[:space_count]
    x_ref, held, turned, sem = refs[space_count:]
    parts, epochs, rows, cols = x_ref.shape
    fetches = [
        pltpu.make_async_copy(x_hbm.at[part, l], x_ref.at[part, l], sem.at[part * epochs + l])
        for part in range(parts)
        for l in range(epochs)
    ]
    for fetch in fetches:
        fetch.start()
    looks = cols // LOOKC
    blocks = looks // GROUP
    width = GROUP * LOOKC
    lines = parts * epochs * rows
    pairs = rows // 2
    own = lax.axis_index("space")

    source = lax.broadcasted_iota(jnp.int32, (width, 2 * LANES), 0)
    lane = lax.broadcasted_iota(jnp.int32, (width, 2 * LANES), 1)
    word = (lane // GROUP) % 8
    k = 2 * (4 * (lane // LANES) + word % 4) + word // 4
    picks = jnp.where((source == (lane % GROUP) * LOOKC + k) & (k < LOOKC), 1.0, 0.0).astype(jnp.bfloat16)
    zeros = jnp.zeros((SUBLANES, LANES), jnp.float32)
    for part in range(parts):
        for at in range(LOOKC):
            for l in range(epochs):
                turned[part, at, l, 0:SUBLANES, :] = zeros
                turned[part, at, l, SUBLANES + pairs : 2 * SUBLANES + pairs, :] = zeros
    for fetch in fetches:
        fetch.wait()
    x = x_ref[...].reshape(lines, cols)
    turned_blocks = [
        jnp.dot(x[:, j * width : (j + 1) * width], picks, preferred_element_type=jnp.float32)
        for j in range(blocks)
    ]
    place = (lax.broadcasted_iota(jnp.int32, (lines, LANES), 1) // GROUP) % 4
    half = lax.broadcasted_iota(jnp.int32, (lines // 2, LANES), 1) < LANES // 2
    for kp in range((LOOKC + 1) // 2):
        column = kp // 4
        merged = None
        for j in range(blocks):
            piece = turned_blocks[j][:, column * LANES : (column + 1) * LANES]
            shift = (GROUP * (j - kp % 4)) % LANES
            if shift:
                piece = pltpu.roll(piece, shift, 1)
            merged = piece if merged is None else jnp.where(place == j, piece, merged)
        held[kp] = merged
        even = held[kp, pl.ds(0, lines // 2, stride=2), :]
        odd = held[kp, pl.ds(1, lines // 2, stride=2), :]
        first = jnp.where(half, even, pltpu.roll(odd, LANES // 2, 1))
        second = jnp.where(half, pltpu.roll(even, LANES // 2, 1), odd)
        for at, value in ((2 * kp, first), (2 * kp + 1, second)):
            if at >= LOOKC:
                continue
            for part in range(parts):
                for l in range(epochs):
                    g = part * epochs + l
                    turned[part, at, l, SUBLANES : SUBLANES + pairs, :] = value[g * pairs : (g + 1) * pairs]
    taken = outs[0].shape[2] // epochs
    for j in range(space_count):
        start = SUBLANES - 1 + (own ^ j) * (taken - MARGIN)
        for part in range(parts):
            for at in range(LOOKC):
                tile = [turned[part, at, l, pl.ds(start, taken), :] for l in range(epochs)]
                tile = tile[0] if epochs == 1 else jnp.concatenate(tile, axis=0)
                outs[j][part, at] = tile.astype(jnp.bfloat16)


def pack_kernel(*refs):
    out = refs[-1]
    for n, piece in enumerate(refs[:-1]):
        out[n] = piece[...]


def windowed(values, h, high):
    a, b, c = values[h], values[h + 1], values[h + 2]
    return a + b + c + pltpu.roll(b + jnp.where(high, a, c), LANES // 2, 1)


def stage_kernel(plan, *refs):
    space_count, epochs, taken = plan["space"], plan["epochs"], plan["taken"]
    build, tasks, finish, first, last = (plan[n] for n in ("build", "tasks", "finish", "first", "last"))
    pieces = {
        name: refs[at] if slot is None else refs[at].at[slot] for name, (at, slot) in plan["places"].items()
    }
    refs = refs[plan["operands"] :]
    if not first:
        refs = refs[4:]
    if last:
        out_hbm, refs = refs[0], refs[1:]
    left, sums, powers, ready = refs[:4]
    own_power = refs[4]
    group = epochs * space_count
    lines = epochs * taken
    own = lax.axis_index("space")
    block_own = lax.axis_index("epoch")
    blocks = ready.shape[0]

    def send(m):
        row = pl.multiple_of((block_own ^ m) * group, group)
        return pltpu.make_async_copy(ready.at[m], out_hbm.at[:, :, pl.ds(row, group), :], refs[5].at[m])

    if last:
        for m in range(blocks):
            if m not in finish:
                send(m).start()

    for j in build:
        piece = pieces[0, j]

        def lift(k, carry):
            for part in range(2):
                tile = piece[part, k].astype(jnp.float32)
                for l in range(epochs):
                    half = tile[l * taken : (l + 1) * taken]
                    if epochs > 1:
                        half = jnp.concatenate([half] * epochs, axis=0)
                    left[k, part, (own ^ j) * epochs + l] = half
            return carry

        lax.fori_loop(0, LOOKC, lift, 0)

    for m, j, sources in tasks:
        piece = pieces[m, j]
        chosen = [(own ^ s) * epochs + l for s in sources for l in range(epochs)]
        count = len(chosen)
        zero = jnp.zeros((lines, LANES), jnp.float32)

        def add(step, carry):
            carry = list(carry)
            for inner in range(3):
                k = step * 3 + inner
                right_re = piece[0, k].astype(jnp.float32)
                right_im = piece[1, k].astype(jnp.float32)
                carry[2 * count] = carry[2 * count] + (right_re * right_re + right_im * right_im)
                for n, e in enumerate(chosen):
                    left_re = left[k, 0, e]
                    left_im = left[k, 1, e]
                    carry[2 * n] = carry[2 * n] + (left_re * right_re + left_im * right_im)
                    carry[2 * n + 1] = carry[2 * n + 1] + (left_im * right_re - left_re * right_im)
            return tuple(carry)

        total = lax.fori_loop(0, LOOKC // 3, add, (zero,) * (2 * count + 1))
        row = pl.multiple_of((own ^ j) * SUBLANES, SUBLANES)
        for n, e in enumerate(chosen):
            for part in range(2):
                sums[m, part, e, pl.ds(row, lines), :] = total[2 * n + part]
        powers[m, pl.ds(row, lines), :] = total[2 * count]

    stride = SUBLANES // epochs
    high = lax.broadcasted_iota(jnp.int32, (group, LANES), 1) >= LANES // 2

    def power_of(m, h):
        return windowed([powers[m, pl.ds(q, group, stride=stride), :] for q in range(taken)], h, high) + 1e-06

    if finish:
        for h in range(taken - MARGIN):
            own_power[h] = power_of(0, h)
    for m in finish:
        power = [power_of(m, h) for h in range(taken - MARGIN)]
        for e in range(group):
            inverse = [lax.rsqrt(own_power[h, pl.ds(e, 1), :] * power[h]) for h in range(taken - MARGIN)]
            for part in range(2):
                values = [sums[m, part, e, pl.ds(q, group, stride=stride), :] for q in range(taken)]
                for h in range(taken - MARGIN):
                    ready[m, part, e, :, h * LANES : (h + 1) * LANES] = (
                        windowed(values, h, high) * inverse[h]
                    ).astype(jnp.bfloat16)
        if last:
            send(m).start()
    if last:
        for m in range(blocks):
            send(m).wait()


def swapped(value, axis, mask):
    count = lax.axis_size(axis)
    return lax.ppermute(value, axis, [(a, a ^ mask) for a in range(count)])


def stages_of(space_count, epoch_count):
    every = tuple(range(space_count))
    if space_count == 4 and epoch_count == 4:
        return [[(int(n[0]), int(n[1]), tuple(map(int, n[2:])) or every) for n in stage] for stage in STAGES]
    tail = (epoch_count - 2, space_count - 1)
    stages = [[], [tail + (every,)], [(tail[0] + 1, tail[1], every)]]
    for m in range(epoch_count):
        for j in range(space_count):
            if (m - m % 2, j) != tail:
                stages[m % 2].append((m, j, every))
    return stages


def straight_of(space_count, epoch_count):
    return [(int(n[0]), int(n[1])) for n in STRAIGHT] if space_count == 4 and epoch_count == 4 else []


def groups_of(space_count, epoch_count):
    if space_count == 4 and epoch_count == 4:
        return [[(int(n[0]), int(n[1])) for n in group] for group in GROUPS]
    keys = [(m, j) for m in range(0, epoch_count, 2) for j in range(space_count)]
    return [keys[:-1], keys[-1:]]


def per_device(slc_stack):
    parts, epochs, rows, cols = slc_stack.shape
    space_count = lax.axis_size("space")
    epoch_count = lax.axis_size("epoch")
    strip_rows = rows // space_count
    looks = cols // LOOKC
    taken = strip_rows // 2 + MARGIN
    group = epochs * space_count
    lines = epochs * taken
    vmem = pl.BlockSpec(memory_space=pltpu.VMEM)
    params = pltpu.CompilerParams(vmem_limit_bytes=GRANT)

    strips = pl.pallas_call(
        functools.partial(split_kernel, space_count),
        out_shape=[jax.ShapeDtypeStruct((parts, LOOKC, lines, LANES), jnp.bfloat16)] * space_count,
        in_specs=[pl.BlockSpec(memory_space=pltpu.HBM)],
        out_specs=[vmem] * space_count,
        scratch_shapes=[
            pltpu.VMEM(slc_stack.shape, slc_stack.dtype),
            pltpu.VMEM(((LOOKC + 1) // 2, parts * epochs * rows, LANES), jnp.float32),
            pltpu.VMEM((parts, LOOKC, epochs, rows // 2 + 2 * SUBLANES, LANES), jnp.float32),
            pltpu.SemaphoreType.DMA((parts * epochs,)),
        ],
        compiler_params=params,
        name="split",
    )(pltpu.with_memory_space_constraint(slc_stack, pltpu.HBM))

    blocks = {0: [strips[0]] + [swapped(strips[j], "space", j) for j in range(1, space_count)]}
    bit = epoch_count // 2
    while bit > 1:
        for mask in list(blocks):
            flip = bit | int(bit in CROSS)
            blocks[mask ^ flip] = [swapped(p, "epoch", flip) for p in blocks[mask]]
        bit //= 2
    found = {(m, j): (piece, None) for m in blocks for j, piece in enumerate(blocks[m])}
    for m, j in straight_of(space_count, epoch_count):
        found[m, j] = (swapped(blocks[0][j], "epoch", m), None)
    for keys in groups_of(space_count, epoch_count):
        taken_pieces = [blocks[m][j] for m, j in keys]
        if len(keys) == 1:
            array = swapped(taken_pieces[0], "epoch", 1)
            found[keys[0][0] ^ 1, keys[0][1]] = (array, None)
            continue
        array = pl.pallas_call(
            pack_kernel,
            out_shape=jax.ShapeDtypeStruct((len(keys), parts, LOOKC, lines, LANES), jnp.bfloat16),
            in_specs=[vmem] * len(keys),
            out_specs=vmem,
            compiler_params=params,
            cost_estimate=pl.CostEstimate(
                flops=0, bytes_accessed=len(keys) * parts * LOOKC * lines * LANES, transcendentals=0
            ),
        )(*taken_pieces)
        array = swapped(array, "epoch", 1)
        found.update({(m ^ 1, j): (array, n) for n, (m, j) in enumerate(keys)})

    state_shapes = [
        jax.ShapeDtypeStruct((LOOKC, parts, group, lines, LANES), jnp.float32),
        jax.ShapeDtypeStruct((epoch_count, parts, group, space_count * SUBLANES, LANES), jnp.float32),
        jax.ShapeDtypeStruct((epoch_count, space_count * SUBLANES, LANES), jnp.float32),
        jax.ShapeDtypeStruct((epoch_count, parts, group, group, strip_rows * looks), jnp.bfloat16),
    ]
    out_shape = jax.ShapeDtypeStruct((parts, group, group * epoch_count, strip_rows * looks), jnp.bfloat16)
    stages = stages_of(space_count, epoch_count)
    built, done, finished = set(), set(), set()
    state = ()
    out = None
    for number, tasks in enumerate(stages):
        first, last = number == 0, number == len(stages) - 1
        build = sorted({s for _, _, sources in tasks for s in sources} - built)
        built |= set(build)
        done |= {(m, j, s) for m, j, sources in tasks for s in sources}
        full = [
            m
            for m in range(epoch_count)
            if all((m, j, s) in done for j in range(space_count) for s in range(space_count))
        ]
        finish = [m for m in full if m not in finished] if 0 in full else []
        finished |= set(finish)
        arrays, places = [], {}
        for name in sorted(set([(0, j) for j in build] + [(m, j) for m, j, _ in tasks])):
            array, slot = found[name]
            at = next((n for n, a in enumerate(arrays) if a is array), len(arrays))
            arrays += [array] if at == len(arrays) else []
            places[name] = (at, slot)
        plan = dict(
            space=space_count, epochs=epochs, taken=taken, build=build, tasks=tasks, finish=finish,
            first=first, last=last, places=places, operands=len(arrays),
        )
        work = sum(len(sources) for _, _, sources in tasks)
        results = pl.pallas_call(
            functools.partial(stage_kernel, plan),
            out_shape=([out_shape] if last else []) + state_shapes,
            in_specs=[vmem] * (len(arrays) + len(state)),
            out_specs=([pl.BlockSpec(memory_space=pl.ANY)] if last else []) + [vmem] * 4,
            input_output_aliases={len(arrays) + n: n + int(last) for n in range(len(state))},
            scratch_shapes=[pltpu.VMEM((taken - MARGIN, group, LANES), jnp.float32)]
            + ([pltpu.SemaphoreType.DMA((epoch_count,))] if last else []),
            compiler_params=params,
            cost_estimate=pl.CostEstimate(
                flops=8 * work * epochs * lines * LOOKC * LANES,
                bytes_accessed=len(places) * parts * LOOKC * lines * LANES * 2,
                transcendentals=0,
            ),
        )(*arrays, *state)
        if last:
            out, results = results[0], results[1:]
        state = tuple(results)
    return out


CROSS = ()
STRAIGHT = ('33',)
GROUPS = (('00', '01', '02', '03', '20', '21'), ('22',))
STAGES = (('0001', '0101'), ('0023', '0123', '02', '03', '20', '21', '22'), ('10', '11', '12', '13', '30', '31'), ('32', '23'), ('33',))


def solution(mesh):
    in_specs = (P(None, ("epoch", "space"), "groups", None),)
    out_specs = P(None, "epoch", None, ("groups", "space"))

    return jax.shard_map(per_device, mesh=mesh, in_specs=in_specs, out_specs=out_specs, check_vma=False)
```

```python
import functools

import jax
import jax.numpy as jnp
from jax import lax
from jax.experimental import pallas as pl
from jax.experimental.pallas import tpu as pltpu
from jax.sharding import PartitionSpec as P

LOOKC = 15
MARGIN = 2
LANES = 128
SUBLANES = 8
GROUP = 16
GRANT = 8 << 20


def split_kernel(space_count, x_hbm, *refs):
    outs = refs[:space_count]
    x_ref, held, turned, sem = refs[space_count:]
    parts, epochs, rows, cols = x_ref.shape
    fetches = [
        pltpu.make_async_copy(x_hbm.at[part, l], x_ref.at[part, l], sem.at[part * epochs + l])
        for part in range(parts)
        for l in range(epochs)
    ]
    for fetch in fetches:
        fetch.start()
    looks = cols // LOOKC
    blocks = looks // GROUP
    width = GROUP * LOOKC
    lines = parts * epochs * rows
    pairs = rows // 2
    own = lax.axis_index("space")

    source = lax.broadcasted_iota(jnp.int32, (width, 2 * LANES), 0)
    lane = lax.broadcasted_iota(jnp.int32, (width, 2 * LANES), 1)
    word = (lane // GROUP) % 8
    k = 2 * (4 * (lane // LANES) + word % 4) + word // 4
    picks = jnp.where((source == (lane % GROUP) * LOOKC + k) & (k < LOOKC), 1.0, 0.0).astype(jnp.bfloat16)
    zeros = jnp.zeros((SUBLANES, LANES), jnp.float32)
    for part in range(parts):
        for at in range(LOOKC):
            for l in range(epochs):
                turned[part, at, l, 0:SUBLANES, :] = zeros
                turned[part, at, l, SUBLANES + pairs : 2 * SUBLANES + pairs, :] = zeros
    for fetch in fetches:
        fetch.wait()
    x = x_ref[...].reshape(lines, cols)
    turned_blocks = [
        jnp.dot(x[:, j * width : (j + 1) * width], picks, preferred_element_type=jnp.float32)
        for j in range(blocks)
    ]
    place = (lax.broadcasted_iota(jnp.int32, (lines, LANES), 1) // GROUP) % 4
    half = lax.broadcasted_iota(jnp.int32, (lines // 2, LANES), 1) < LANES // 2
    merged_all = []
    for column in range(2):
        words = [t[:, column * LANES : (column + 1) * LANES] for t in turned_blocks]
        for bit in (1, 2):
            words = [
                jnp.where(
                    (place & bit) == (j & bit),
                    words[j],
                    pltpu.roll(words[j ^ bit], LANES - bit * GROUP if j & bit else bit * GROUP, 1),
                )
                for j in range(blocks)
            ]
        merged_all += words
    for kp in range((LOOKC + 1) // 2):
        merged = merged_all[kp]
        held[kp] = merged
        even = held[kp, pl.ds(0, lines // 2, stride=2), :]
        odd = held[kp, pl.ds(1, lines // 2, stride=2), :]
        first = jnp.where(half, even, pltpu.roll(odd, LANES // 2, 1))
        second = jnp.where(half, pltpu.roll(even, LANES // 2, 1), odd)
        for at, value in ((2 * kp, first), (2 * kp + 1, second)):
            if at >= LOOKC:
                continue
            for part in range(parts):
                for l in range(epochs):
                    g = part * epochs + l
                    turned[part, at, l, SUBLANES : SUBLANES + pairs, :] = value[g * pairs : (g + 1) * pairs]
    taken = outs[0].shape[2] // epochs
    for j in range(space_count):
        start = SUBLANES - 1 + (own ^ j) * (taken - MARGIN)
        for part in range(parts):
            for at in range(LOOKC):
                tile = [turned[part, at, l, pl.ds(start, taken), :] for l in range(epochs)]
                tile = tile[0] if epochs == 1 else jnp.concatenate(tile, axis=0)
                outs[j][part, at] = tile.astype(jnp.bfloat16)


def pack_kernel(*refs):
    out = refs[-1]
    for n, piece in enumerate(refs[:-1]):
        out[n] = piece[...]


def windowed(values, h, high):
    a, b, c = values[h], values[h + 1], values[h + 2]
    return a + b + c + pltpu.roll(b + jnp.where(high, a, c), LANES // 2, 1)


def stage_kernel(plan, *refs):
    space_count, epochs, taken = plan["space"], plan["epochs"], plan["taken"]
    build, tasks, finish, first, last = (plan[n] for n in ("build", "tasks", "finish", "first", "last"))
    pieces = {
        name: refs[at] if slot is None else refs[at].at[slot] for name, (at, slot) in plan["places"].items()
    }
    refs = refs[plan["operands"] :]
    if not first:
        refs = refs[4:]
    if last:
        out_hbm, refs = refs[0], refs[1:]
    left, sums, powers, ready = refs[:4]
    own_power = refs[4]
    group = epochs * space_count
    lines = epochs * taken
    own = lax.axis_index("space")
    block_own = lax.axis_index("epoch")
    blocks = ready.shape[0]

    def send(m):
        row = pl.multiple_of((block_own ^ m) * group, group)
        return pltpu.make_async_copy(ready.at[m], out_hbm.at[:, :, pl.ds(row, group), :], refs[5].at[m])

    if last:
        for m in range(blocks):
            if m not in finish:
                send(m).start()

    for j in build:
        piece = pieces[0, j]

        def lift(k, carry):
            for part in range(2):
                tile = piece[part, k].astype(jnp.float32)
                for l in range(epochs):
                    half = tile[l * taken : (l + 1) * taken]
                    if epochs > 1:
                        half = jnp.concatenate([half] * epochs, axis=0)
                    left[k, part, (own ^ j) * epochs + l] = half
            return carry

        lax.fori_loop(0, LOOKC, lift, 0)

    for m, j, sources in tasks:
        piece = pieces[m, j]
        chosen = [(own ^ s) * epochs + l for s in sources for l in range(epochs)]
        count = len(chosen)
        zero = jnp.zeros((lines, LANES), jnp.float32)

        def add(step, carry):
            carry = list(carry)
            for inner in range(3):
                k = step * 3 + inner
                right_re = piece[0, k].astype(jnp.float32)
                right_im = piece[1, k].astype(jnp.float32)
                carry[2 * count] = carry[2 * count] + (right_re * right_re + right_im * right_im)
                for n, e in enumerate(chosen):
                    left_re = left[k, 0, e]
                    left_im = left[k, 1, e]
                    carry[2 * n] = carry[2 * n] + (left_re * right_re + left_im * right_im)
                    carry[2 * n + 1] = carry[2 * n + 1] + (left_im * right_re - left_re * right_im)
            return tuple(carry)

        total = lax.fori_loop(0, LOOKC // 3, add, (zero,) * (2 * count + 1))
        row = pl.multiple_of((own ^ j) * SUBLANES, SUBLANES)
        for n, e in enumerate(chosen):
            for part in range(2):
                sums[m, part, e, pl.ds(row, lines), :] = total[2 * n + part]
        for at, s in enumerate(sources):
            if m or s == j:
                continue
            other = pl.multiple_of((own ^ s) * SUBLANES, SUBLANES)
            for part in range(2):
                tiles = [total[2 * (at * epochs + l) + part] for l in range(epochs)]
                for l in range(epochs):
                    tile = [t[l * taken : (l + 1) * taken] for t in tiles]
                    tile = tile[0] if epochs == 1 else jnp.concatenate(tile, axis=0)
                    sums[m, part, (own ^ j) * epochs + l, pl.ds(other, lines), :] = -tile if part else tile
        powers[m, pl.ds(row, lines), :] = total[2 * count]

    stride = SUBLANES // epochs
    high = lax.broadcasted_iota(jnp.int32, (group, LANES), 1) >= LANES // 2

    def power_of(m, h):
        return windowed([powers[m, pl.ds(q, group, stride=stride), :] for q in range(taken)], h, high) + 1e-06

    if finish:
        for h in range(taken - MARGIN):
            own_power[h] = power_of(0, h)
    for m in finish:
        power = [power_of(m, h) for h in range(taken - MARGIN)]
        for e in range(group):
            inverse = [lax.rsqrt(own_power[h, pl.ds(e, 1), :] * power[h]) for h in range(taken - MARGIN)]
            for part in range(2):
                values = [sums[m, part, e, pl.ds(q, group, stride=stride), :] for q in range(taken)]
                for h in range(taken - MARGIN):
                    ready[m, part, e, :, h * LANES : (h + 1) * LANES] = (
                        windowed(values, h, high) * inverse[h]
                    ).astype(jnp.bfloat16)
        if last:
            send(m).start()
    if last:
        for m in range(blocks):
            send(m).wait()


def swapped(value, axis, mask):
    count = lax.axis_size(axis)
    return lax.ppermute(value, axis, [(a, a ^ mask) for a in range(count)])


def stages_of(space_count, epoch_count):
    every = tuple(range(space_count))
    if space_count == 4 and epoch_count == 4:
        return [[(int(n[0]), int(n[1]), tuple(map(int, n[2:])) or every) for n in stage] for stage in STAGES]
    tail = (epoch_count - 2, space_count - 1)
    stages = [[], [tail + (every,)], [(tail[0] + 1, tail[1], every)]]
    for m in range(epoch_count):
        for j in range(space_count):
            if (m - m % 2, j) != tail:
                stages[m % 2].append((m, j, every if m else every[: j + 1]))
    return stages


def straight_of(space_count, epoch_count):
    return [(int(n[0]), int(n[1])) for n in STRAIGHT] if space_count == 4 and epoch_count == 4 else []


def groups_of(space_count, epoch_count):
    if space_count == 4 and epoch_count == 4:
        return [[(int(n[0]), int(n[1])) for n in group] for group in GROUPS]
    keys = [(m, j) for m in range(0, epoch_count, 2) for j in range(space_count)]
    return [keys[:-1], keys[-1:]]


def per_device(slc_stack):
    parts, epochs, rows, cols = slc_stack.shape
    space_count = lax.axis_size("space")
    epoch_count = lax.axis_size("epoch")
    strip_rows = rows // space_count
    looks = cols // LOOKC
    taken = strip_rows // 2 + MARGIN
    group = epochs * space_count
    lines = epochs * taken
    vmem = pl.BlockSpec(memory_space=pltpu.VMEM)
    params = pltpu.CompilerParams(vmem_limit_bytes=GRANT)

    strips = pl.pallas_call(
        functools.partial(split_kernel, space_count),
        out_shape=[jax.ShapeDtypeStruct((parts, LOOKC, lines, LANES), jnp.bfloat16)] * space_count,
        in_specs=[pl.BlockSpec(memory_space=pltpu.HBM)],
        out_specs=[vmem] * space_count,
        scratch_shapes=[
            pltpu.VMEM(slc_stack.shape, slc_stack.dtype),
            pltpu.VMEM(((LOOKC + 1) // 2, parts * epochs * rows, LANES), jnp.float32),
            pltpu.VMEM((parts, LOOKC, epochs, rows // 2 + 2 * SUBLANES, LANES), jnp.float32),
            pltpu.SemaphoreType.DMA((parts * epochs,)),
        ],
        compiler_params=params,
        name="split",
    )(pltpu.with_memory_space_constraint(slc_stack, pltpu.HBM))

    blocks = {0: [strips[0]] + [swapped(strips[j], "space", j) for j in range(1, space_count)]}
    bit = epoch_count // 2
    while bit > 1:
        for mask in list(blocks):
            flip = bit | int(bit in CROSS)
            blocks[mask ^ flip] = [swapped(p, "epoch", flip) for p in blocks[mask]]
        bit //= 2
    found = {(m, j): (piece, None) for m in blocks for j, piece in enumerate(blocks[m])}
    for m, j in straight_of(space_count, epoch_count):
        found[m, j] = (swapped(blocks[0][j], "epoch", m), None)
    for keys in groups_of(space_count, epoch_count):
        taken_pieces = [blocks[m][j] for m, j in keys]
        if len(keys) == 1:
            array = swapped(taken_pieces[0], "epoch", 1)
            found[keys[0][0] ^ 1, keys[0][1]] = (array, None)
            continue
        array = pl.pallas_call(
            pack_kernel,
            out_shape=jax.ShapeDtypeStruct((len(keys), parts, LOOKC, lines, LANES), jnp.bfloat16),
            in_specs=[vmem] * len(keys),
            out_specs=vmem,
            compiler_params=params,
            cost_estimate=pl.CostEstimate(
                flops=0, bytes_accessed=len(keys) * parts * LOOKC * lines * LANES, transcendentals=0
            ),
        )(*taken_pieces)
        array = swapped(array, "epoch", 1)
        found.update({(m ^ 1, j): (array, n) for n, (m, j) in enumerate(keys)})

    state_shapes = [
        jax.ShapeDtypeStruct((LOOKC, parts, group, lines, LANES), jnp.float32),
        jax.ShapeDtypeStruct((epoch_count, parts, group, space_count * SUBLANES, LANES), jnp.float32),
        jax.ShapeDtypeStruct((epoch_count, space_count * SUBLANES, LANES), jnp.float32),
        jax.ShapeDtypeStruct((epoch_count, parts, group, group, strip_rows * looks), jnp.bfloat16),
    ]
    out_shape = jax.ShapeDtypeStruct((parts, group, group * epoch_count, strip_rows * looks), jnp.bfloat16)
    stages = stages_of(space_count, epoch_count)
    built, done, finished = set(), set(), set()
    state = ()
    out = None
    for number, tasks in enumerate(stages):
        first, last = number == 0, number == len(stages) - 1
        build = sorted({s for _, _, sources in tasks for s in sources} - built)
        built |= set(build)
        done |= {(m, j, s) for m, j, sources in tasks for s in sources}
        done |= {(0, s, j) for m, j, sources in tasks for s in sources if m == 0}
        full = [
            m
            for m in range(epoch_count)
            if all((m, j, s) in done for j in range(space_count) for s in range(space_count))
        ]
        finish = [m for m in full if m not in finished] if 0 in full else []
        finished |= set(finish)
        arrays, places = [], {}
        for name in sorted(set([(0, j) for j in build] + [(m, j) for m, j, _ in tasks])):
            array, slot = found[name]
            at = next((n for n, a in enumerate(arrays) if a is array), len(arrays))
            arrays += [array] if at == len(arrays) else []
            places[name] = (at, slot)
        plan = dict(
            space=space_count, epochs=epochs, taken=taken, build=build, tasks=tasks, finish=finish,
            first=first, last=last, places=places, operands=len(arrays),
        )
        work = sum(len(sources) for _, _, sources in tasks)
        results = pl.pallas_call(
            functools.partial(stage_kernel, plan),
            out_shape=([out_shape] if last else []) + state_shapes,
            in_specs=[vmem] * (len(arrays) + len(state)),
            out_specs=([pl.BlockSpec(memory_space=pl.ANY)] if last else []) + [vmem] * 4,
            input_output_aliases={len(arrays) + n: n + int(last) for n in range(len(state))},
            scratch_shapes=[pltpu.VMEM((taken - MARGIN, group, LANES), jnp.float32)]
            + ([pltpu.SemaphoreType.DMA((epoch_count,))] if last else []),
            compiler_params=params,
            cost_estimate=pl.CostEstimate(
                flops=8 * work * epochs * lines * LOOKC * LANES,
                bytes_accessed=len(places) * parts * LOOKC * lines * LANES * 2,
                transcendentals=0,
            ),
        )(*arrays, *state)
        if last:
            out, results = results[0], results[1:]
        state = tuple(results)
    return out


CROSS = ()
STRAIGHT = ('33',)
GROUPS = (('00', '01', '02', '03', '20', '21'), ('22',))
STAGES = (('000', '0101'), ('02012', '03', '20', '21', '22'), ('10', '11', '12', '13', '30', '31'), ('32', '23'), ('33',))


def solution(mesh):
    in_specs = (P(None, ("epoch", "space"), "groups", None),)
    out_specs = P(None, "epoch", None, ("groups", "space"))

    return jax.shard_map(per_device, mesh=mesh, in_specs=in_specs, out_specs=out_specs, check_vma=False)
```

```python
import functools

import jax
import jax.numpy as jnp
from jax import lax
from jax.experimental import pallas as pl
from jax.experimental.pallas import tpu as pltpu
from jax.sharding import PartitionSpec as P

LOOKC = 15
MARGIN = 2
LANES = 128
SUBLANES = 8
GROUP = 16
GRANT = 8 << 20


def split_kernel(space_count, x_hbm, *refs):
    outs = refs[:space_count]
    x_ref, held, turned, sem = refs[space_count:]
    parts, epochs, rows, cols = x_ref.shape
    fetches = [
        pltpu.make_async_copy(x_hbm.at[part, l], x_ref.at[part, l], sem.at[part * epochs + l])
        for part in range(parts)
        for l in range(epochs)
    ]
    for fetch in fetches:
        fetch.start()
    looks = cols // LOOKC
    blocks = looks // GROUP
    width = GROUP * LOOKC
    lines = parts * epochs * rows
    pairs = rows // 2
    own = lax.axis_index("space")

    source = lax.broadcasted_iota(jnp.int32, (width, 2 * LANES), 0)
    lane = lax.broadcasted_iota(jnp.int32, (width, 2 * LANES), 1)
    word = (lane // GROUP) % 8
    k = 2 * (4 * (lane // LANES) + word % 4) + word // 4
    picks = jnp.where((source == (lane % GROUP) * LOOKC + k) & (k < LOOKC), 1.0, 0.0).astype(jnp.bfloat16)
    zeros = jnp.zeros((SUBLANES, LANES), jnp.float32)
    for part in range(parts):
        for at in range(LOOKC):
            for l in range(epochs):
                turned[part, at, l, 0:SUBLANES, :] = zeros
                turned[part, at, l, SUBLANES + pairs : 2 * SUBLANES + pairs, :] = zeros
    for fetch in fetches:
        fetch.wait()
    x = x_ref[...].reshape(lines, cols)
    turned_blocks = [
        jnp.dot(x[:, j * width : (j + 1) * width], picks, preferred_element_type=jnp.float32)
        for j in range(blocks)
    ]
    place = (lax.broadcasted_iota(jnp.int32, (lines, LANES), 1) // GROUP) % 4
    half = lax.broadcasted_iota(jnp.int32, (lines // 2, LANES), 1) < LANES // 2
    merged_all = []
    for column in range(2):
        words = [t[:, column * LANES : (column + 1) * LANES] for t in turned_blocks]
        for bit in (1, 2):
            words = [
                jnp.where(
                    (place & bit) == (j & bit),
                    words[j],
                    pltpu.roll(words[j ^ bit], LANES - bit * GROUP if j & bit else bit * GROUP, 1),
                )
                for j in range(blocks)
            ]
        merged_all += words
    for kp in range((LOOKC + 1) // 2):
        merged = merged_all[kp]
        held[kp] = merged
        even = held[kp, pl.ds(0, lines // 2, stride=2), :]
        odd = held[kp, pl.ds(1, lines // 2, stride=2), :]
        first = jnp.where(half, even, pltpu.roll(odd, LANES // 2, 1))
        second = jnp.where(half, pltpu.roll(even, LANES // 2, 1), odd)
        for at, value in ((2 * kp, first), (2 * kp + 1, second)):
            if at >= LOOKC:
                continue
            for part in range(parts):
                for l in range(epochs):
                    g = part * epochs + l
                    turned[part, at, l, SUBLANES : SUBLANES + pairs, :] = value[g * pairs : (g + 1) * pairs]
    taken = outs[0].shape[2] // epochs
    for j in range(space_count):
        start = SUBLANES - 1 + (own ^ j) * (taken - MARGIN)
        for part in range(parts):
            for at in range(LOOKC):
                tile = [turned[part, at, l, pl.ds(start, taken), :] for l in range(epochs)]
                tile = tile[0] if epochs == 1 else jnp.concatenate(tile, axis=0)
                outs[j][part, at] = tile.astype(jnp.bfloat16)


def pack_kernel(*refs):
    out = refs[-1]
    for n, piece in enumerate(refs[:-1]):
        out[n] = piece[...]


def windowed(values, h, high):
    a, b, c = values[h], values[h + 1], values[h + 2]
    return a + b + c + pltpu.roll(b + jnp.where(high, a, c), LANES // 2, 1)


def stage_kernel(plan, *refs):
    space_count, epochs, taken = plan["space"], plan["epochs"], plan["taken"]
    build, tasks, finish, first, last = (plan[n] for n in ("build", "tasks", "finish", "first", "last"))
    pieces = {
        name: refs[at] if slot is None else refs[at].at[slot] for name, (at, slot) in plan["places"].items()
    }
    refs = refs[plan["operands"] :]
    if not first:
        refs = refs[4:]
    if last:
        out_hbm, refs = refs[0], refs[1:]
    left, sums, powers, ready = refs[:4]
    own_power = refs[4]
    group = epochs * space_count
    lines = epochs * taken
    own = lax.axis_index("space")
    block_own = lax.axis_index("epoch")
    blocks = ready.shape[0]

    def send(m):
        row = pl.multiple_of((block_own ^ m) * group, group)
        return pltpu.make_async_copy(ready.at[m], out_hbm.at[:, :, pl.ds(row, group), :], refs[5].at[m])

    if last:
        for m in range(blocks):
            if m not in finish:
                send(m).start()

    for j in build:
        piece = pieces[0, j]

        def lift(k, carry):
            for part in range(2):
                tile = piece[part, k].astype(jnp.float32)
                for l in range(epochs):
                    half = tile[l * taken : (l + 1) * taken]
                    if epochs > 1:
                        half = jnp.concatenate([half] * epochs, axis=0)
                    left[k, part, (own ^ j) * epochs + l] = half
            return carry

        lax.fori_loop(0, LOOKC, lift, 0)

    for m, j, sources in tasks:
        piece = pieces[m, j]
        chosen = [(own ^ s) * epochs + l for s in sources for l in range(epochs)]
        count = len(chosen)
        zero = jnp.zeros((lines, LANES), jnp.float32)

        def add(step, carry):
            carry = list(carry)
            for inner in range(3):
                k = step * 3 + inner
                right_re = piece[0, k].astype(jnp.float32)
                right_im = piece[1, k].astype(jnp.float32)
                carry[2 * count] = carry[2 * count] + (right_re * right_re + right_im * right_im)
                for n, e in enumerate(chosen):
                    left_re = left[k, 0, e]
                    left_im = left[k, 1, e]
                    carry[2 * n] = carry[2 * n] + (left_re * right_re + left_im * right_im)
                    carry[2 * n + 1] = carry[2 * n + 1] + (left_im * right_re - left_re * right_im)
            return tuple(carry)

        total = lax.fori_loop(0, LOOKC // 3, add, (zero,) * (2 * count + 1))
        row = pl.multiple_of((own ^ j) * SUBLANES, SUBLANES)
        for n, e in enumerate(chosen):
            for part in range(2):
                sums[m, part, e, pl.ds(row, lines), :] = total[2 * n + part]
        for at, s in enumerate(sources):
            if m or s == j:
                continue
            other = pl.multiple_of((own ^ s) * SUBLANES, SUBLANES)
            for part in range(2):
                tiles = [total[2 * (at * epochs + l) + part] for l in range(epochs)]
                for l in range(epochs):
                    tile = [t[l * taken : (l + 1) * taken] for t in tiles]
                    tile = tile[0] if epochs == 1 else jnp.concatenate(tile, axis=0)
                    sums[m, part, (own ^ j) * epochs + l, pl.ds(other, lines), :] = -tile if part else tile
        powers[m, pl.ds(row, lines), :] = total[2 * count]

    stride = SUBLANES // epochs
    high = lax.broadcasted_iota(jnp.int32, (group, LANES), 1) >= LANES // 2

    def power_of(m, h):
        return windowed([powers[m, pl.ds(q, group, stride=stride), :] for q in range(taken)], h, high) + 1e-06

    if finish:
        for h in range(taken - MARGIN):
            own_power[h] = power_of(0, h)
    for m in finish:
        power = [power_of(m, h) for h in range(taken - MARGIN)]
        for e in range(group):
            inverse = [lax.rsqrt(own_power[h, pl.ds(e, 1), :] * power[h]) for h in range(taken - MARGIN)]
            for part in range(2):
                values = [sums[m, part, e, pl.ds(q, group, stride=stride), :] for q in range(taken)]
                for h in range(taken - MARGIN):
                    ready[m, part, e, :, h * LANES : (h + 1) * LANES] = (
                        windowed(values, h, high) * inverse[h]
                    ).astype(jnp.bfloat16)
        if last:
            send(m).start()
    if last:
        for m in range(blocks):
            send(m).wait()


def swapped(value, axis, mask):
    count = lax.axis_size(axis)
    return lax.ppermute(value, axis, [(a, a ^ mask) for a in range(count)])


def stages_of(space_count, epoch_count):
    every = tuple(range(space_count))
    if space_count == 4 and epoch_count == 4:
        return [[(int(n[0]), int(n[1]), tuple(map(int, n[2:])) or every) for n in stage] for stage in STAGES]
    tail = (epoch_count - 2, space_count - 1)
    stages = [[], [tail + (every,)], [(tail[0] + 1, tail[1], every)]]
    for m in range(epoch_count):
        for j in range(space_count):
            if (m - m % 2, j) != tail:
                stages[m % 2].append((m, j, every if m else every[: j + 1]))
    return stages


def straight_of(space_count, epoch_count):
    return [(int(n[0]), int(n[1])) for n in STRAIGHT] if space_count == 4 and epoch_count == 4 else []


def groups_of(space_count, epoch_count):
    if space_count == 4 and epoch_count == 4:
        return [[(int(n[0]), int(n[1])) for n in group] for group in GROUPS]
    keys = [(m, j) for m in range(0, epoch_count, 2) for j in range(space_count)]
    return [keys[:-1], keys[-1:]]


def per_device(slc_stack):
    parts, epochs, rows, cols = slc_stack.shape
    space_count = lax.axis_size("space")
    epoch_count = lax.axis_size("epoch")
    strip_rows = rows // space_count
    looks = cols // LOOKC
    taken = strip_rows // 2 + MARGIN
    group = epochs * space_count
    lines = epochs * taken
    vmem = pl.BlockSpec(memory_space=pltpu.VMEM)
    params = pltpu.CompilerParams(vmem_limit_bytes=GRANT)

    strips = pl.pallas_call(
        functools.partial(split_kernel, space_count),
        out_shape=[jax.ShapeDtypeStruct((parts, LOOKC, lines, LANES), jnp.bfloat16)] * space_count,
        in_specs=[pl.BlockSpec(memory_space=pltpu.HBM)],
        out_specs=[vmem] * space_count,
        scratch_shapes=[
            pltpu.VMEM(slc_stack.shape, slc_stack.dtype),
            pltpu.VMEM(((LOOKC + 1) // 2, parts * epochs * rows, LANES), jnp.float32),
            pltpu.VMEM((parts, LOOKC, epochs, rows // 2 + 2 * SUBLANES, LANES), jnp.float32),
            pltpu.SemaphoreType.DMA((parts * epochs,)),
        ],
        compiler_params=params,
        name="split",
    )(pltpu.with_memory_space_constraint(slc_stack, pltpu.HBM))

    blocks = {0: [strips[0]] + [swapped(strips[j], "space", j) for j in range(1, space_count)]}
    bit = epoch_count // 2
    while bit > 1:
        for mask in list(blocks):
            flip = bit | int(bit in CROSS)
            blocks[mask ^ flip] = [swapped(p, "epoch", flip) for p in blocks[mask]]
        bit //= 2
    found = {(m, j): (piece, None) for m in blocks for j, piece in enumerate(blocks[m])}
    for m, j in straight_of(space_count, epoch_count):
        found[m, j] = (swapped(blocks[0][j], "epoch", m), None)
    for keys in groups_of(space_count, epoch_count):
        taken_pieces = [blocks[m][j] for m, j in keys]
        if len(keys) == 1:
            array = swapped(taken_pieces[0], "epoch", 1)
            found[keys[0][0] ^ 1, keys[0][1]] = (array, None)
            continue
        array = pl.pallas_call(
            pack_kernel,
            out_shape=jax.ShapeDtypeStruct((len(keys), parts, LOOKC, lines, LANES), jnp.bfloat16),
            in_specs=[vmem] * len(keys),
            out_specs=vmem,
            compiler_params=params,
            cost_estimate=pl.CostEstimate(
                flops=0, bytes_accessed=len(keys) * parts * LOOKC * lines * LANES, transcendentals=0
            ),
        )(*taken_pieces)
        array = swapped(array, "epoch", 1)
        found.update({(m ^ 1, j): (array, n) for n, (m, j) in enumerate(keys)})

    state_shapes = [
        jax.ShapeDtypeStruct((LOOKC, parts, group, lines, LANES), jnp.float32),
        jax.ShapeDtypeStruct((epoch_count, parts, group, space_count * SUBLANES, LANES), jnp.float32),
        jax.ShapeDtypeStruct((epoch_count, space_count * SUBLANES, LANES), jnp.float32),
        jax.ShapeDtypeStruct((epoch_count, parts, group, group, strip_rows * looks), jnp.bfloat16),
    ]
    out_shape = jax.ShapeDtypeStruct((parts, group, group * epoch_count, strip_rows * looks), jnp.bfloat16)
    stages = stages_of(space_count, epoch_count)
    built, done, finished = set(), set(), set()
    state = ()
    out = None
    for number, tasks in enumerate(stages):
        first, last = number == 0, number == len(stages) - 1
        build = sorted({s for _, _, sources in tasks for s in sources} - built)
        built |= set(build)
        done |= {(m, j, s) for m, j, sources in tasks for s in sources}
        done |= {(0, s, j) for m, j, sources in tasks for s in sources if m == 0}
        full = [
            m
            for m in range(epoch_count)
            if all((m, j, s) in done for j in range(space_count) for s in range(space_count))
        ]
        finish = [m for m in full if m not in finished] if 0 in full else []
        finished |= set(finish)
        arrays, places = [], {}
        for name in sorted(set([(0, j) for j in build] + [(m, j) for m, j, _ in tasks])):
            array, slot = found[name]
            at = next((n for n, a in enumerate(arrays) if a is array), len(arrays))
            arrays += [array] if at == len(arrays) else []
            places[name] = (at, slot)
        plan = dict(
            space=space_count, epochs=epochs, taken=taken, build=build, tasks=tasks, finish=finish,
            first=first, last=last, places=places, operands=len(arrays),
        )
        work = sum(len(sources) for _, _, sources in tasks)
        results = pl.pallas_call(
            functools.partial(stage_kernel, plan),
            out_shape=([out_shape] if last else []) + state_shapes,
            in_specs=[vmem] * (len(arrays) + len(state)),
            out_specs=([pl.BlockSpec(memory_space=pl.ANY)] if last else []) + [vmem] * 4,
            input_output_aliases={len(arrays) + n: n + int(last) for n in range(len(state))},
            scratch_shapes=[pltpu.VMEM((taken - MARGIN, group, LANES), jnp.float32)]
            + ([pltpu.SemaphoreType.DMA((epoch_count,))] if last else []),
            compiler_params=params,
            cost_estimate=pl.CostEstimate(
                flops=8 * work * epochs * lines * LOOKC * LANES,
                bytes_accessed=len(places) * parts * LOOKC * lines * LANES * 2,
                transcendentals=0,
            ),
        )(*arrays, *state)
        if last:
            out, results = results[0], results[1:]
        state = tuple(results)
    return out


CROSS = ()
STRAIGHT = ('33',)
GROUPS = (('00', '01', '02', '03', '20', '21'), ('22',))
STAGES = (
    ("000", "0101"),
    ("02012",),
    ("03", "20", "21", "22"),
    ("10", "11", "12", "13", "30", "31"),
    ("32", "23"),
    ("33",),
)


def solution(mesh):
    in_specs = (P(None, ("epoch", "space"), "groups", None),)
    out_specs = P(None, "epoch", None, ("groups", "space"))

    return jax.shard_map(per_device, mesh=mesh, in_specs=in_specs, out_specs=out_specs, check_vma=False)
```
